128 devices in a mesh: tm: 16 (over y, z), env: 8 (over x, core).
Axes of the slice: x: 4, y: 4, z: 4, core: 2. Of those that a mesh axis runs over, the one named last changes fastest.
Arguments:
- rewards: float32 [32768, 4096], P('tm', 'env'), may hold values from -0.16 to 0.16
- values: float32 [32768, 4096], P('tm', 'env'), may hold values from -6 to 6
- last_value: float32 [4096], P('env'), may hold values from -6 to 6
- done_steps: int32 [4096, 4], P('env'), may hold values from 0 to 32767
- horizon_offset: int32 [4096], P('env'), may hold values from 0 to 16383
- discount_rate: float32 [4096], P('env'), may hold values from 1.5258789e-06 to 0.03
- trace_rate: float32 [4096], P('env'), may hold values from 1.5258789e-06 to 0.03
Outputs:
- norm_advantages: float32 [4096, 32768], P(('env', 'tm'))
- norm_returns: float32 [4096, 32768], P(('env', 'tm'))
The draws below stay inside these ranges and needn't reach their ends.
Inputs may be any that keep to these rules, and one draw needn't show every extreme that they name: `done_steps`: a repeated step in one environment's list is one termination.
All inputs are finite; a program needn't handle non-finite values.
Results may differ from the reference program's by a relative error of at most 0.0008.
Values sent between devices are 32-bit elements; how exact they have to be, the bound alone decides.
No kernel may reach another device: no remote copies, remote signals or barrier semaphores. Data moves between devices by JAX's collectives and lax.ppermute only.
A program may use at most 128 MiB of HBM per device.

```python
import math
import jax
import jax.numpy as jnp
from jax import lax

EVENTS = 4
TSTEPS = 32768
ENVS = 4096
HORIZON = 16384


def touch_ends(result, rng, smallest, high):
    shape = result.shape
    spot = [jax.random.randint(jax.random.fold_in(rng, axis), (), 0, shape[axis]) for axis in range(len(shape))]
    result = result.at[tuple(spot)].set(smallest)
    longest = shape.index(max(shape))
    spot[longest] = (spot[longest] + 1) % shape[longest]
    return result.at[tuple(spot)].set(high)


def block_scale(own_key, dims, shards, least, largest):
    def one(axis_at, blocks):
        steps = jax.random.uniform(jax.random.fold_in(jax.random.fold_in(own_key, 6), axis_at), (blocks,), jnp.float32, least / len(shards), largest / len(shards))
        return jnp.repeat(jnp.exp(steps), dims[axis_at] // blocks).reshape((-1,) + (1,) * (len(dims) - axis_at - 1))

    loudness = one(*shards[0])
    for cut in shards[1:]:
        loudness = loudness * one(*cut)
    return loudness


def noise(key, shape, width, reach, cuts=(), kind=jnp.bfloat16):
    array = width * jax.random.normal(key, shape, jnp.float32)
    if cuts:
        array = array * block_scale(key, shape, cuts, -0.22, 0.18)
    return jnp.clip(array, -reach, reach).astype(kind)


def setup_inputs(seed: int = 0) -> dict:
    key_of = jax.random.split(jax.random.key(seed), 8)
    rewards = noise(key_of[0], (TSTEPS, ENVS), 0.02, 0.16, ((0, 16), (1, 8)), jnp.float32)
    values = noise(key_of[1], (TSTEPS, ENVS), 1.0, 6.0, ((0, 16), (1, 8)), jnp.float32)
    last_value = noise(key_of[2], (ENVS,), 1.0, 6.0, ((0, 8),), jnp.float32)
    done_steps = touch_ends(jax.random.randint(key_of[3], (ENVS, EVENTS), 0, TSTEPS), jax.random.fold_in(key_of[3], 1), 0, TSTEPS - 1).astype(jnp.int32)
    horizon_offset = touch_ends(jax.random.randint(key_of[4], (ENVS,), 0, HORIZON), jax.random.fold_in(key_of[4], 1), 0, HORIZON - 1).astype(jnp.int32)
    discount_rate = jnp.clip(jnp.exp(math.log(0.03) - 9.886382 * jax.random.uniform(key_of[5], (ENVS,), jnp.float32) ** block_scale(key_of[5], (ENVS,), ((0, 8),), -0.2, 0.2)), 1.5258789289873675e-06, 0.03)
    trace_rate = jnp.clip(jnp.exp(math.log(0.03) - 9.886382 * jax.random.uniform(key_of[6], (ENVS,), jnp.float32) ** block_scale(key_of[6], (ENVS,), ((0, 8),), -0.2, 0.2)), 1.5258789289873675e-06, 0.03)
    return dict(rewards=rewards, values=values, last_value=last_value, done_steps=done_steps, horizon_offset=horizon_offset, discount_rate=discount_rate, trace_rate=trace_rate)


def normalize(field):
    center = jnp.mean(field)
    spread = jnp.mean((field - center) * (field - center))
    return (field - center) / jnp.sqrt(spread + 1e-05)

def reference(rewards, values, last_value, done_steps, horizon_offset, discount_rate, trace_rate):
    moment_index = jnp.arange(TSTEPS, dtype=jnp.int32)
    discount = jnp.exp(-discount_rate)
    retention = discount * jnp.exp(-trace_rate)

    def backward(state, inputs):
        adv_next, value_next = state
        reward, value, moment = inputs
        finished = jnp.any(done_steps == moment, axis=1)
        truncated = (moment + horizon_offset) % HORIZON == HORIZON - 1
        living = 1.0 - finished.astype(rewards.dtype)
        carried = living * (1.0 - truncated.astype(rewards.dtype))
        td_error = reward + discount * living * value_next - value
        advantage = td_error + retention * carried * adv_next
        return ((advantage, value), advantage)
    start_state = (jnp.zeros_like(last_value), last_value)
    unused, advantages = lax.scan(backward, start_state, (rewards, values, moment_index), reverse=True)
    returns = advantages + values
    return (normalize(advantages).T, normalize(returns).T)
```

```python
import functools

import jax
import jax.numpy as jnp
from jax import lax
from jax.experimental import pallas as pl
from jax.experimental.pallas import tpu as pltpu
from jax.sharding import Mesh
from jax.sharding import PartitionSpec as P

TM = ("tm_0", "tm_1")
ENV = ("env_0", "env_1")
ALL = ("tm_0", "tm_1", "env_0", "env_1")
ENV_TM = ("env_0", "env_1", "tm_0", "tm_1")
F32 = jnp.float32
LANES = 128
SEG = 32
ROWS = 256
SMEM = pl.BlockSpec(memory_space=pltpu.SMEM)
ANY = pl.BlockSpec(memory_space=pl.ANY)


def params(**kw):
    return pltpu.CompilerParams(vmem_limit_bytes=56 << 20, **kw)


def cost(flops, moved):
    return pl.CostEstimate(flops=flops, transcendentals=0, bytes_accessed=moved)


def pack_body(dests, riders, *refs):
    x_ref, o_ref = refs[0], refs[-1]
    own = x_ref.shape[1] // dests
    base = pl.program_id(0) * (ROWS // LANES) * own if riders else 0
    for h in range(ROWS // LANES):
        tile = x_ref[h * LANES : (h + 1) * LANES, :].T.reshape(dests, own, LANES)
        if riders:
            o_ref[:, pl.ds(pl.multiple_of(base + h * own, own), own), :] = tile
        else:
            o_ref[:, h * own : (h + 1) * own, :] = tile
    if riders:

        @pl.when(pl.program_id(0) == 0)
        def _():
            lines = refs[1][...]
            o_ref[:, o_ref.shape[1] - riders :, :] = jnp.broadcast_to(
                lines[None], (dests, *lines.shape)
            )


def pack(block, dests, start, count, rider=None):
    envs = block.shape[1]
    own = envs // dests
    riders = 0 if rider is None else rider.shape[0]
    rows = count // LANES * own
    per = ROWS // LANES * own
    in_specs = [pl.BlockSpec((ROWS, envs), lambda i: (start // ROWS + i, 0))]
    if riders:
        in_specs.append(pl.BlockSpec(rider.shape, lambda i: (0, 0)))
        out_spec = pl.BlockSpec((dests, rows + riders, LANES), lambda i: (0, 0, 0))
    else:
        out_spec = pl.BlockSpec((dests, per, LANES), lambda i: (0, i, 0))
    return pl.pallas_call(
        functools.partial(pack_body, dests, riders),
        grid=(count // ROWS,),
        in_specs=in_specs,
        out_specs=out_spec,
        out_shape=jax.ShapeDtypeStruct((dests, rows + riders, LANES), F32),
        compiler_params=params(),
        cost_estimate=cost(0, 8 * count * envs),
        name="pack",
    )(block, *(() if rider is None else (rider,)))


def stepper(rew_ref, val_ref, times_ref, rates_ref, length):
    first = lax.broadcasted_iota(jnp.int32, (SEG, LANES), 0) * length
    marks = [
        jnp.broadcast_to(times_ref[k : k + 1, :], (8, LANES))
        for k in range(times_ref.shape[0])
    ]
    marks = [jnp.concatenate([m] * (SEG // 8), axis=0) for m in marks]
    discount = jnp.broadcast_to(rates_ref[0:1, :], (SEG, LANES))
    retention = jnp.broadcast_to(rates_ref[1:2, :], (SEG, LANES))

    def step(i, next_value):
        rows = pl.ds(i, SEG, stride=length)
        reward, value = rew_ref[rows, :], val_ref[rows, :]
        time = first + i
        ended = marks[0] == time
        for mark in marks[1:-1]:
            ended = ended | (mark == time)
        follow = jnp.where(ended, 0.0, discount)
        decay = jnp.where(ended | (marks[-1] == time), 0.0, retention)
        td_error = reward + follow * next_value - value
        return value, td_error, decay, follow

    return step


def value_after(val_ref, boundary, length):
    firsts = val_ref[pl.ds(0, SEG, stride=length), :]
    return jnp.concatenate([firsts[1:], boundary], axis=0)


def summary_body(length, rew_ref, val_ref, times_ref, rates_ref, seg_ref, all_ref):
    step = stepper(rew_ref, val_ref, times_ref, rates_ref, length)
    zero = jnp.zeros((SEG, LANES), F32)

    following = value_after(val_ref, zero[:1], length)
    value, partial, last_decay, last_follow = step(length - 1, following)

    def body(k, carry):
        partial, product, following = carry
        value, td_error, decay, _ = step(length - 2 - k, following)
        return td_error + decay * partial, decay * product, value

    partial, product, _ = lax.fori_loop(
        0, length - 1, body, (partial, zero + 1.0, value), unroll=7
    )
    coefs = product * last_follow
    product = product * last_decay
    seg_ref[0] = partial
    seg_ref[1] = product
    seg_ref[2] = coefs
    s = SEG - 1
    own, kept, coef = partial[s:], product[s:], coefs[s:]
    for s in range(SEG - 2, -1, -1):
        factor = product[s : s + 1]
        own = partial[s : s + 1] + factor * own
        kept = factor * kept
        coef = factor * coef
    lines = jnp.concatenate([own, kept, coef, val_ref[0:1, :]], axis=0)
    all_ref[pl.ds(4 * pl.program_id(0), 4), :] = lines


def columns(*lead):
    return pl.BlockSpec((*lead, LANES), lambda j: (*(0 for _ in lead), j))


def summary(rewards, values, times, rates):
    steps, envs = rewards.shape
    groups = envs // LANES
    return pl.pallas_call(
        functools.partial(summary_body, steps // SEG),
        grid=(groups,),
        in_specs=[columns(steps), columns(steps), columns(len(times)), columns(2)],
        out_specs=[columns(3, SEG), pl.BlockSpec((4 * groups, LANES), lambda j: (0, 0))],
        out_shape=[
            jax.ShapeDtypeStruct((3, SEG, envs), F32),
            jax.ShapeDtypeStruct((4 * groups, LANES), F32),
        ],
        compiler_params=params(),
        cost_estimate=cost(16 * steps * envs, 8 * steps * envs),
        name="summary",
    )(rewards, values, times, rates)


def advantage_body(
    length, here_ref, rew_ref, val_ref, times_ref, rates_ref, last_ref, seg_ref, every_ref, adv_ref, stat_ref
):
    steps = rew_ref.shape[0]
    group = pl.program_id(0)
    here = here_ref[0]
    step = stepper(rew_ref, val_ref, times_ref, rates_ref, length)

    boundary = last_ref[...]
    incoming = jnp.zeros((1, LANES), F32)
    for s in range(every_ref.shape[0] - 1, 0, -1):
        lines = every_ref[s, pl.ds(4 * group, 4), :]
        later = here < s
        start = (lines[0:1] + lines[2:3] * boundary) + lines[1:2] * incoming
        incoming = jnp.where(later, start, incoming)
        boundary = jnp.where(later, lines[3:4], boundary)

    partial, product = seg_ref[0], seg_ref[1]
    after = [incoming]
    for s in range(SEG - 1, 0, -1):
        own = partial[s : s + 1]
        if s == SEG - 1:
            own = own + seg_ref[2, s : s + 1, :] * boundary
        after.append(own + product[s : s + 1] * after[-1])
    after = jnp.concatenate(after[::-1], axis=0)

    def body(k, carry):
        later, following, sum_adv, sum_val = carry
        i = length - 1 - k
        value, td_error, decay, _ = step(i, following)
        own = td_error + decay * later
        adv_ref[pl.ds(i, SEG, stride=length), :] = own
        return own, value, sum_adv + own, sum_val + value

    zero = jnp.zeros((SEG, LANES), F32)
    start = (after, value_after(val_ref, boundary, length), zero, zero)
    _, _, sum_adv, sum_val = lax.fori_loop(0, length, body, start, unroll=8)
    sums = [jnp.sum(sum_adv), jnp.sum(sum_adv + sum_val)]
    mean_adv, mean_ret = [total / (steps * LANES) for total in sums]

    zero = jnp.zeros((64, LANES), F32)

    def spread(k, carry):
        sq_adv, sq_ret = carry
        rows = pl.ds(pl.multiple_of(k * 64, 64), 64)
        own = adv_ref[rows, :]
        off_adv = own - mean_adv
        off_ret = (own + val_ref[rows, :]) - mean_ret
        return sq_adv + off_adv * off_adv, sq_ret + off_ret * off_ret

    sq_adv, sq_ret = lax.fori_loop(0, steps // 64, spread, (zero, zero), unroll=2)
    sums += [jnp.sum(sq_adv), jnp.sum(sq_ret)]
    lane = lax.broadcasted_iota(jnp.int32, stat_ref.shape, 1)

    @pl.when(group == 0)
    def _():
        stat_ref[...] = jnp.zeros(stat_ref.shape, F32)

    line = stat_ref[...]
    for k, total in enumerate(sums):
        line = jnp.where(lane == 4 * group + k, total, line)
    stat_ref[...] = line


def advantage(here, rewards, values, times, rates, last_value, segments, every):
    steps, envs = rewards.shape
    return pl.pallas_call(
        functools.partial(advantage_body, steps // SEG),
        grid=(envs // LANES,),
        in_specs=[
            SMEM, columns(steps), columns(steps), columns(len(times)), columns(2), columns(1),
            columns(3, SEG), pl.BlockSpec(every.shape, lambda j: (0, 0, 0)),
        ],
        out_specs=[columns(steps), pl.BlockSpec((8, LANES), lambda j: (0, 0))],
        out_shape=[
            jax.ShapeDtypeStruct((steps, envs), F32),
            jax.ShapeDtypeStruct((8, LANES), F32),
        ],
        compiler_params=params(),
        cost_estimate=cost(24 * steps * envs, 12 * steps * envs),
        name="advantage",
    )(here, rewards, values, times, rates, last_value, segments, every)


def normal_body(counts, steps, offset, stat_ref, adv, *refs):
    vals = refs[: len(counts)]
    out_adv, out_ret, abuf, vbuf, oabuf, orbuf, in_sem, out_sem = refs[-8:]
    blocks, rows, _ = abuf.shape
    own = out_adv.shape[0]
    width = rows // own * LANES

    def fetches(s):
        copies = [pltpu.make_async_copy(adv.at[s, pl.ds(0, rows)], abuf.at[s], in_sem.at[0, s])]
        at = 0
        for k, (val, count) in enumerate(zip(vals, counts)):
            copies.append(
                pltpu.make_async_copy(
                    val.at[s, pl.ds(0, count)], vbuf.at[s, pl.ds(at, count)], in_sem.at[k + 1, s]
                )
            )
            at += count
        return copies

    def stores(s):
        place = pl.ds(pl.multiple_of(s * steps + offset, LANES), width)
        return [
            pltpu.make_async_copy(buf.at[s], out.at[:, place], out_sem.at[k, s])
            for k, (buf, out) in enumerate(((oabuf, out_adv), (orbuf, out_ret)))
        ]

    def each(body):
        lax.fori_loop(0, blocks, lambda s, c: (body(s), c)[1], 0)

    def begin(s):
        for copy in fetches(s):
            copy.start()

    def work(s):
        for copy in fetches(s):
            copy.wait()
        for h in range(rows // own):
            part = abuf[s, h * own : (h + 1) * own, :]
            ret = part + vbuf[s, h * own : (h + 1) * own, :]
            lanes = slice(h * LANES, (h + 1) * LANES)
            oabuf[s, :, lanes] = (part - stat_ref[0]) * stat_ref[1]
            orbuf[s, :, lanes] = (ret - stat_ref[2]) * stat_ref[3]
        for copy in stores(s):
            copy.start()

    def finish(s):
        for copy in stores(s):
            copy.wait()

    each(begin)
    each(work)
    each(finish)


def normalized(stats, adv, vals, counts, own, steps, offset, into=None):
    blocks, rows = adv.shape[0], sum(counts)
    shape = jax.ShapeDtypeStruct((own, blocks * steps), F32)
    into = () if into is None else tuple(into)
    at = 2 + len(vals)
    width = rows // own * LANES
    return pl.pallas_call(
        functools.partial(normal_body, counts, steps, offset),
        in_specs=[SMEM] + [ANY] * (1 + len(vals) + len(into)),
        out_specs=[ANY, ANY],
        out_shape=[shape, shape],
        input_output_aliases={at + k: k for k in range(len(into))},
        scratch_shapes=[
            pltpu.VMEM((blocks, rows, LANES), F32),
            pltpu.VMEM((blocks, rows, LANES), F32),
            pltpu.VMEM((blocks, own, width), F32),
            pltpu.VMEM((blocks, own, width), F32),
            pltpu.SemaphoreType.DMA((1 + len(vals), blocks)),
            pltpu.SemaphoreType.DMA((2, blocks)),
        ],
        compiler_params=params(),
        cost_estimate=cost(4 * blocks * rows * LANES, 16 * blocks * rows * LANES),
        name="normalized",
    )(stats, adv, *vals, *into)


def exchange(packed, behind=None):
    if behind is not None:
        packed, behind = lax.optimization_barrier((packed, behind))
    return lax.all_to_all(packed, TM, 0, 0, tiled=True), behind


def merged(mean, square, count, axis, distance):
    size = lax.axis_size(axis)
    other = lax.ppermute(
        jnp.concatenate([mean, square]), axis, [(i, (i + distance) % size) for i in range(size)]
    )
    gap = other[:2] - mean
    return mean + 0.5 * gap, square + other[2:] + (0.5 * count) * gap * gap, 2.0 * count


def shards(rewards, values, last_value, done_steps, horizon_offset, discount_rate, trace_rate):
    steps, envs = rewards.shape
    blocks = lax.axis_size(TM)
    here = lax.axis_index(TM)
    horizon = steps * blocks // 2
    groups = envs // LANES
    own = envs // blocks
    half, quarter = steps // 2, steps // 4
    rows = lambda count: count // LANES * own

    val_1, _ = exchange(pack(values, blocks, 0, quarter))

    discount = jnp.exp(-discount_rate)
    rates = jnp.stack([discount, discount * jnp.exp(-trace_rate)])
    truncated = jnp.mod(horizon - 1 - horizon_offset - here * steps, horizon)
    times = jnp.concatenate([done_steps.T - here * steps, truncated[None]], axis=0)
    segments, whole = summary(rewards, values, times, rates)

    val_2, val_1 = exchange(pack(values, blocks, quarter, quarter, whole), val_1)
    val_3, val_2 = exchange(pack(values, blocks, half, half), val_2)
    every = val_2[:, rows(quarter) :, :]
    adv, local = advantage(
        here.reshape(1), rewards, values, times, rates, last_value[None], segments, every
    )
    adv_1, val_3 = exchange(pack(adv, blocks, 0, half, local), val_3)
    adv_2, adv_1 = exchange(pack(adv, blocks, half, half), adv_1)

    parts = adv_1[:, rows(half), : 4 * groups].reshape(-1, 4)
    count = float(steps * LANES)
    means = parts[:, :2] / count
    mean = jnp.mean(means, axis=0)
    off = means - mean
    square = jnp.sum(parts[:, 2:] + count * off * off, axis=0)
    count = count * groups * blocks
    mean, square, count = merged(mean, square, count, ENV[1], 1)
    mean, square, count = merged(mean, square, count, ENV[0], 1)
    mean, square, count = merged(mean, square, count, ENV[0], 2)
    scale = 1.0 / jnp.sqrt(square / count + 1e-05)
    stats = jnp.stack([mean[0], scale[0], mean[1], scale[1]])

    counts = (rows(quarter), rows(quarter))
    out = normalized(stats, adv_1, (val_1, val_2), counts, own, steps, 0)
    return tuple(normalized(stats, adv_2, (val_3,), (rows(half),), own, steps, half, out))


def solution(mesh):
    split = Mesh(mesh.devices.reshape(4, 4, 4, 2), ALL)
    placed = (P(TM, ENV), P(TM, ENV), P(ENV), P(ENV, None), P(ENV), P(ENV), P(ENV))
    return jax.shard_map(
        shards,
        mesh=split,
        in_specs=placed,
        out_specs=(P(ENV_TM, None), P(ENV_TM, None)),
        check_vma=False,
    )
```

```python
import functools

import jax
import jax.numpy as jnp
from jax import lax
from jax.experimental import pallas as pl
from jax.experimental.pallas import tpu as pltpu
from jax.sharding import Mesh
from jax.sharding import PartitionSpec as P

TM = ("tm_0", "tm_1")
ENV = ("env_0", "env_1")
ALL = ("tm_0", "tm_1", "env_0", "env_1")
ENV_TM = ("env_0", "env_1", "tm_0", "tm_1")
F32 = jnp.float32
LANES = 128
SEG = 32
ROWS = 256
SMEM = pl.BlockSpec(memory_space=pltpu.SMEM)
ANY = pl.BlockSpec(memory_space=pl.ANY)


def params(**kw):
    return pltpu.CompilerParams(vmem_limit_bytes=56 << 20, **kw)


def cost(flops, moved):
    return pl.CostEstimate(flops=flops, transcendentals=0, bytes_accessed=moved)


def pack_body(dests, riders, *refs):
    x_ref, o_ref = refs[0], refs[-1]
    own = x_ref.shape[1] // dests
    base = pl.program_id(0) * (ROWS // LANES) * own if riders else 0
    for h in range(ROWS // LANES):
        tile = x_ref[h * LANES : (h + 1) * LANES, :].T.reshape(dests, own, LANES)
        if riders:
            o_ref[:, pl.ds(pl.multiple_of(base + h * own, own), own), :] = tile
        else:
            o_ref[:, h * own : (h + 1) * own, :] = tile
    if riders:

        @pl.when(pl.program_id(0) == 0)
        def _():
            lines = refs[1][...]
            o_ref[:, o_ref.shape[1] - riders :, :] = jnp.broadcast_to(
                lines[None], (dests, *lines.shape)
            )


def pack(block, dests, start, count, rider=None):
    envs = block.shape[1]
    own = envs // dests
    riders = 0 if rider is None else rider.shape[0]
    rows = count // LANES * own
    per = ROWS // LANES * own
    in_specs = [pl.BlockSpec((ROWS, envs), lambda i: (start // ROWS + i, 0))]
    if riders:
        in_specs.append(pl.BlockSpec(rider.shape, lambda i: (0, 0)))
        out_spec = pl.BlockSpec((dests, rows + riders, LANES), lambda i: (0, 0, 0))
    else:
        out_spec = pl.BlockSpec((dests, per, LANES), lambda i: (0, i, 0))
    return pl.pallas_call(
        functools.partial(pack_body, dests, riders),
        grid=(count // ROWS,),
        in_specs=in_specs,
        out_specs=out_spec,
        out_shape=jax.ShapeDtypeStruct((dests, rows + riders, LANES), F32),
        compiler_params=params(),
        cost_estimate=cost(0, 8 * count * envs),
        name="pack",
    )(block, *(() if rider is None else (rider,)))


def stepper(times_ref, rates_ref, length):
    first = lax.broadcasted_iota(jnp.int32, (SEG, LANES), 0) * length
    marks = [times_ref[k : k + 1, :] for k in range(times_ref.shape[0])]
    discount, retention = rates_ref[0:1, :], rates_ref[1:2, :]

    def step(i, reward, value, next_value):
        time = first + i
        ended = marks[0] == time
        for mark in marks[1:-1]:
            ended = ended | (mark == time)
        follow = jnp.where(ended, 0.0, discount)
        decay = jnp.where(ended | (marks[-1] == time), 0.0, retention)
        return reward + follow * next_value - value, decay, follow

    return step


def by_step(ref, at):
    return jnp.swapaxes(ref[:, pl.ds(pl.multiple_of(at, 8), 8), :], 0, 1)


def value_after(val_ref, boundary):
    firsts = jnp.swapaxes(val_ref[:, 0:8, :], 0, 1)[0]
    return jnp.concatenate([firsts[1:], boundary], axis=0)


def summary_body(rew_ref, val_ref, times_ref, rates_ref, seg_ref, all_ref):
    length = rew_ref.shape[1]
    step = stepper(times_ref, rates_ref, length)
    zero = jnp.zeros((SEG, LANES), F32)

    def eight(at, partial, product, following, last):
        rewards, values = by_step(rew_ref, at), by_step(val_ref, at)
        for k in range(7, -1, -1):
            td_error, decay, follow = step(at + k, rewards[k], values[k], following)
            if last and k == 7:
                partial, kept = td_error, (decay, follow)
            else:
                partial, product = td_error + decay * partial, decay * product
            following = values[k]
        return (partial, product, following), (kept if last else None)

    carry, (last_decay, last_follow) = eight(
        length - 8, zero, zero + 1.0, value_after(val_ref, zero[:1]), True
    )
    partial, product, following = lax.fori_loop(
        1, length // 8, lambda k, c: eight(length - 8 - 8 * k, *c, False)[0], carry
    )
    coefs = product * last_follow
    product = product * last_decay
    seg_ref[0] = partial
    seg_ref[1] = product
    seg_ref[2] = coefs
    s = SEG - 1
    own, kept, coef = partial[s:], product[s:], coefs[s:]
    for s in range(SEG - 2, -1, -1):
        factor = product[s : s + 1]
        own = partial[s : s + 1] + factor * own
        kept = factor * kept
        coef = factor * coef
    lines = jnp.concatenate([own, kept, coef, following[0:1]], axis=0)
    all_ref[pl.ds(4 * pl.program_id(0), 4), :] = lines


def columns(*lead):
    return pl.BlockSpec((*lead, LANES), lambda j: (*(0 for _ in lead), j))


def segmented(block):
    steps, envs = block.shape
    return block.reshape(SEG, steps // SEG, envs)


def summary(rewards, values, times, rates):
    steps, envs = rewards.shape
    groups = envs // LANES
    return pl.pallas_call(
        summary_body,
        grid=(groups,),
        in_specs=[
            columns(SEG, steps // SEG), columns(SEG, steps // SEG), columns(len(times)), columns(2),
        ],
        out_specs=[columns(3, SEG), pl.BlockSpec((4 * groups, LANES), lambda j: (0, 0))],
        out_shape=[
            jax.ShapeDtypeStruct((3, SEG, envs), F32),
            jax.ShapeDtypeStruct((4 * groups, LANES), F32),
        ],
        compiler_params=params(),
        cost_estimate=cost(16 * steps * envs, 8 * steps * envs),
        name="summary",
    )(segmented(rewards), segmented(values), times, rates)


def advantage_body(
    here_ref, rew_ref, val_ref, times_ref, rates_ref, last_ref, seg_ref, every_ref, adv_ref, stat_ref
):
    length = rew_ref.shape[1]
    group = pl.program_id(0)
    here = here_ref[0]
    step = stepper(times_ref, rates_ref, length)

    boundary = last_ref[...]
    incoming = jnp.zeros((1, LANES), F32)
    for s in range(every_ref.shape[0] - 1, 0, -1):
        lines = every_ref[s, pl.ds(4 * group, 4), :]
        later = here < s
        start = (lines[0:1] + lines[2:3] * boundary) + lines[1:2] * incoming
        incoming = jnp.where(later, start, incoming)
        boundary = jnp.where(later, lines[3:4], boundary)

    partial, product = seg_ref[0], seg_ref[1]
    after = [incoming]
    for s in range(SEG - 1, 0, -1):
        own = partial[s : s + 1]
        if s == SEG - 1:
            own = own + seg_ref[2, s : s + 1, :] * boundary
        after.append(own + product[s : s + 1] * after[-1])
    after = jnp.concatenate(after[::-1], axis=0)

    def body(k, carry):
        later, following, sum_adv, sum_val = carry
        at = length - 8 - 8 * k
        rewards, values = by_step(rew_ref, at), by_step(val_ref, at)
        found = []
        for k in range(7, -1, -1):
            td_error, decay, _ = step(at + k, rewards[k], values[k], following)
            later = td_error + decay * later
            following = values[k]
            found.append(later)
            sum_adv, sum_val = sum_adv + later, sum_val + following
        found = jnp.stack(found[::-1], axis=0)
        adv_ref[:, pl.ds(pl.multiple_of(at, 8), 8), :] = jnp.swapaxes(found, 0, 1)
        return later, following, sum_adv, sum_val

    zero = jnp.zeros((SEG, LANES), F32)
    start = (after, value_after(val_ref, boundary), zero, zero)
    _, _, sum_adv, sum_val = lax.fori_loop(0, length // 8, body, start)
    sums = [jnp.sum(sum_adv), jnp.sum(sum_adv + sum_val)]
    mean_adv, mean_ret = [total / (SEG * length * LANES) for total in sums]

    zero = jnp.zeros((length, LANES), F32)

    def spread(k, carry):
        sq_adv, sq_ret = carry
        own = adv_ref[k]
        off_adv = own - mean_adv
        off_ret = (own + val_ref[k]) - mean_ret
        return sq_adv + off_adv * off_adv, sq_ret + off_ret * off_ret

    sq_adv, sq_ret = lax.fori_loop(0, SEG, spread, (zero, zero), unroll=2)
    sums += [jnp.sum(sq_adv), jnp.sum(sq_ret)]
    lane = lax.broadcasted_iota(jnp.int32, stat_ref.shape, 1)

    @pl.when(group == 0)
    def _():
        stat_ref[...] = jnp.zeros(stat_ref.shape, F32)

    line = stat_ref[...]
    for k, total in enumerate(sums):
        line = jnp.where(lane == 4 * group + k, total, line)
    stat_ref[...] = line


def advantage(here, rewards, values, times, rates, last_value, segments, every):
    steps, envs = rewards.shape
    adv, stats = pl.pallas_call(
        advantage_body,
        grid=(envs // LANES,),
        in_specs=[
            SMEM, columns(SEG, steps // SEG), columns(SEG, steps // SEG), columns(len(times)),
            columns(2), columns(1), columns(3, SEG), pl.BlockSpec(every.shape, lambda j: (0, 0, 0)),
        ],
        out_specs=[columns(SEG, steps // SEG), pl.BlockSpec((8, LANES), lambda j: (0, 0))],
        out_shape=[
            jax.ShapeDtypeStruct((SEG, steps // SEG, envs), F32),
            jax.ShapeDtypeStruct((8, LANES), F32),
        ],
        compiler_params=params(),
        cost_estimate=cost(24 * steps * envs, 12 * steps * envs),
        name="advantage",
    )(here, segmented(rewards), segmented(values), times, rates, last_value, segments, every)
    return adv.reshape(steps, envs), stats


def normal_body(counts, steps, offset, stat_ref, adv, *refs):
    vals = refs[: len(counts)]
    out_adv, out_ret, abuf, vbuf, oabuf, orbuf, in_sem, out_sem = refs[-8:]
    blocks, rows, _ = abuf.shape
    own = out_adv.shape[0]
    width = rows // own * LANES

    def fetches(s):
        copies = [pltpu.make_async_copy(adv.at[s, pl.ds(0, rows)], abuf.at[s], in_sem.at[0, s])]
        at = 0
        for k, (val, count) in enumerate(zip(vals, counts)):
            copies.append(
                pltpu.make_async_copy(
                    val.at[s, pl.ds(0, count)], vbuf.at[s, pl.ds(at, count)], in_sem.at[k + 1, s]
                )
            )
            at += count
        return copies

    def stores(s):
        place = pl.ds(pl.multiple_of(s * steps + offset, LANES), width)
        return [
            pltpu.make_async_copy(buf.at[s], out.at[:, place], out_sem.at[k, s])
            for k, (buf, out) in enumerate(((oabuf, out_adv), (orbuf, out_ret)))
        ]

    def each(body):
        lax.fori_loop(0, blocks, lambda s, c: (body(s), c)[1], 0)

    def begin(s):
        for copy in fetches(s):
            copy.start()

    def work(s):
        for copy in fetches(s):
            copy.wait()
        for h in range(rows // own):
            part = abuf[s, h * own : (h + 1) * own, :]
            ret = part + vbuf[s, h * own : (h + 1) * own, :]
            lanes = slice(h * LANES, (h + 1) * LANES)
            oabuf[s, :, lanes] = (part - stat_ref[0]) * stat_ref[1]
            orbuf[s, :, lanes] = (ret - stat_ref[2]) * stat_ref[3]
        for copy in stores(s):
            copy.start()

    def finish(s):
        for copy in stores(s):
            copy.wait()

    each(begin)
    each(work)
    each(finish)


def normalized(stats, adv, vals, counts, own, steps, offset, into=None):
    blocks, rows = adv.shape[0], sum(counts)
    shape = jax.ShapeDtypeStruct((own, blocks * steps), F32)
    into = () if into is None else tuple(into)
    at = 2 + len(vals)
    width = rows // own * LANES
    return pl.pallas_call(
        functools.partial(normal_body, counts, steps, offset),
        in_specs=[SMEM] + [ANY] * (1 + len(vals) + len(into)),
        out_specs=[ANY, ANY],
        out_shape=[shape, shape],
        input_output_aliases={at + k: k for k in range(len(into))},
        scratch_shapes=[
            pltpu.VMEM((blocks, rows, LANES), F32),
            pltpu.VMEM((blocks, rows, LANES), F32),
            pltpu.VMEM((blocks, own, width), F32),
            pltpu.VMEM((blocks, own, width), F32),
            pltpu.SemaphoreType.DMA((1 + len(vals), blocks)),
            pltpu.SemaphoreType.DMA((2, blocks)),
        ],
        compiler_params=params(),
        cost_estimate=cost(4 * blocks * rows * LANES, 16 * blocks * rows * LANES),
        name="normalized",
    )(stats, adv, *vals, *into)


def exchange(packed, behind=None):
    if behind is not None:
        packed, behind = lax.optimization_barrier((packed, behind))
    return lax.all_to_all(packed, TM, 0, 0, tiled=True), behind


def merged(mean, square, count, axis, distance):
    size = lax.axis_size(axis)
    other = lax.ppermute(
        jnp.concatenate([mean, square]), axis, [(i, (i + distance) % size) for i in range(size)]
    )
    gap = other[:2] - mean
    return mean + 0.5 * gap, square + other[2:] + (0.5 * count) * gap * gap, 2.0 * count


def shards(rewards, values, last_value, done_steps, horizon_offset, discount_rate, trace_rate):
    steps, envs = rewards.shape
    blocks = lax.axis_size(TM)
    here = lax.axis_index(TM)
    horizon = steps * blocks // 2
    groups = envs // LANES
    own = envs // blocks
    half, quarter = steps // 2, steps // 4
    rows = lambda count: count // LANES * own

    discount = jnp.exp(-discount_rate)
    rates = jnp.stack([discount, discount * jnp.exp(-trace_rate)])
    truncated = jnp.mod(horizon - 1 - horizon_offset - here * steps, horizon)
    times = jnp.concatenate([done_steps.T - here * steps, truncated[None]], axis=0)

    core = lax.axis_index(ENV[1])
    given = (rewards, values, times, rates)
    blank = lambda *_: (
        jnp.zeros((3, SEG, envs), F32),
        jnp.zeros((4 * groups, LANES), F32),
    )
    ahead = lax.cond(core == 0, lambda *x: tuple(summary(*x)), blank, *given)
    values_1, ahead = lax.optimization_barrier((values, ahead))
    packed, ahead = lax.optimization_barrier((pack(values_1, blocks, 0, quarter), ahead))
    val_1, _ = exchange(packed)
    segments, whole = lax.cond(
        core == 0, lambda done, *_: done, lambda _, *x: tuple(summary(*x)), ahead, *given
    )

    val_2, val_1 = exchange(pack(values, blocks, quarter, quarter, whole), val_1)
    val_3, val_2 = exchange(pack(values, blocks, half, half), val_2)
    every = val_2[:, rows(quarter) :, :]
    adv, local = advantage(
        here.reshape(1), rewards, values, times, rates, last_value[None], segments, every
    )
    adv_1, val_3 = exchange(pack(adv, blocks, 0, half, local), val_3)
    adv_2, adv_1 = exchange(pack(adv, blocks, half, half), adv_1)

    parts = adv_1[:, rows(half), : 4 * groups].reshape(-1, 4)
    count = float(steps * LANES)
    means = parts[:, :2] / count
    mean = jnp.mean(means, axis=0)
    off = means - mean
    square = jnp.sum(parts[:, 2:] + count * off * off, axis=0)
    count = count * groups * blocks
    mean, square, count = merged(mean, square, count, ENV[1], 1)
    mean, square, count = merged(mean, square, count, ENV[0], 1)
    mean, square, count = merged(mean, square, count, ENV[0], 2)
    scale = 1.0 / jnp.sqrt(square / count + 1e-05)
    stats = jnp.stack([mean[0], scale[0], mean[1], scale[1]])

    counts = (rows(quarter), rows(quarter))
    out = normalized(stats, adv_1, (val_1, val_2), counts, own, steps, 0)
    return tuple(normalized(stats, adv_2, (val_3,), (rows(half),), own, steps, half, out))


def solution(mesh):
    split = Mesh(mesh.devices.reshape(4, 4, 4, 2), ALL)
    placed = (P(TM, ENV), P(TM, ENV), P(ENV), P(ENV, None), P(ENV), P(ENV), P(ENV))
    return jax.shard_map(
        shards,
        mesh=split,
        in_specs=placed,
        out_specs=(P(ENV_TM, None), P(ENV_TM, None)),
        check_vma=False,
    )
```

```python
import functools

import jax
import jax.numpy as jnp
from jax import lax
from jax.experimental import pallas as pl
from jax.experimental.pallas import tpu as pltpu
from jax.sharding import Mesh
from jax.sharding import PartitionSpec as P

TM = ("tm_0", "tm_1")
ENV = ("env_0", "env_1")
ALL = ("tm_0", "tm_1", "env_0", "env_1")
ENV_TM = ("env_0", "env_1", "tm_0", "tm_1")
F32 = jnp.float32
LANES = 128
SEG = 32
ROWS = 256
SMEM = pl.BlockSpec(memory_space=pltpu.SMEM)
ANY = pl.BlockSpec(memory_space=pl.ANY)
VMEM = pl.BlockSpec(memory_space=pltpu.VMEM)


def params(mib=56):
    return pltpu.CompilerParams(vmem_limit_bytes=mib << 20)


def cost(flops, moved):
    return pl.CostEstimate(flops=flops, transcendentals=0, bytes_accessed=moved)


def pack_body(dests, riders, *refs):
    x_ref, o_ref = refs[0], refs[-1]
    own = x_ref.shape[1] // dests
    base = pl.program_id(0) * (ROWS // LANES) * own if riders else 0
    for h in range(ROWS // LANES):
        tile = x_ref[h * LANES : (h + 1) * LANES, :].T.reshape(dests, own, LANES)
        if riders:
            o_ref[:, pl.ds(pl.multiple_of(base + h * own, own), own), :] = tile
        else:
            o_ref[:, h * own : (h + 1) * own, :] = tile
    if riders:

        @pl.when(pl.program_id(0) == 0)
        def _():
            lines = refs[1][...]
            o_ref[:, o_ref.shape[1] - riders :, :] = jnp.broadcast_to(
                lines[None], (dests, *lines.shape)
            )


def pack(block, dests, start, count, rider=None):
    envs = block.shape[1]
    own = envs // dests
    riders = 0 if rider is None else rider.shape[0]
    rows = count // LANES * own
    per = ROWS // LANES * own
    in_specs = [pl.BlockSpec((ROWS, envs), lambda i: (start // ROWS + i, 0))]
    if riders:
        in_specs.append(pl.BlockSpec(rider.shape, lambda i: (0, 0)))
        out_spec = pl.BlockSpec((dests, rows + riders, LANES), lambda i: (0, 0, 0))
    else:
        out_spec = pl.BlockSpec((dests, per, LANES), lambda i: (0, i, 0))
    return pl.pallas_call(
        functools.partial(pack_body, dests, riders),
        grid=(count // ROWS,),
        in_specs=in_specs,
        out_specs=out_spec,
        out_shape=jax.ShapeDtypeStruct((dests, rows + riders, LANES), F32),
        compiler_params=params(),
        cost_estimate=cost(0, 8 * count * envs),
        name="pack",
    )(block, *(() if rider is None else (rider,)))


def stepper(here_ref, done_ref, taken_ref, discount_ref, retention_ref, length):
    first = lax.broadcasted_iota(jnp.int32, (SEG, LANES), 0) * length
    start, horizon = here_ref[0], here_ref[1]
    marks = [done_ref[k : k + 1, :] - start for k in range(done_ref.shape[0])]
    full = horizon - 1 - taken_ref[...] - start
    for _ in range(2):
        full = jnp.where(full < 0, full + horizon, full)
    marks.append(full)
    discount, retention = discount_ref[...], retention_ref[...]

    def step(i, reward, value, next_value):
        time = first + i
        ended = marks[0] == time
        for mark in marks[1:-1]:
            ended = ended | (mark == time)
        follow = jnp.where(ended, 0.0, discount)
        decay = jnp.where(ended | (marks[-1] == time), 0.0, retention)
        return reward + follow * next_value - value, decay, follow

    return step


def by_step(ref, at):
    return jnp.swapaxes(ref[:, pl.ds(pl.multiple_of(at, 8), 8), :], 0, 1)


def value_after(val_ref, boundary):
    firsts = jnp.swapaxes(val_ref[:, 0:8, :], 0, 1)[0]
    return jnp.concatenate([firsts[1:], boundary], axis=0)


def summary_body(here_ref, rew_ref, val_ref, *refs):
    seg_ref, all_ref = refs[-2:]
    length = rew_ref.shape[1]
    step = stepper(here_ref, *refs[:4], length)
    zero = jnp.zeros((SEG, LANES), F32)

    def eight(at, partial, product, following, last):
        rewards, values = by_step(rew_ref, at), by_step(val_ref, at)
        for k in range(7, -1, -1):
            td_error, decay, follow = step(at + k, rewards[k], values[k], following)
            if last and k == 7:
                partial, kept = td_error, (decay, follow)
            else:
                partial, product = td_error + decay * partial, decay * product
            following = values[k]
        return (partial, product, following), (kept if last else None)

    carry, (last_decay, last_follow) = eight(
        length - 8, zero, zero + 1.0, value_after(val_ref, zero[:1]), True
    )
    partial, product, following = lax.fori_loop(
        1, length // 8, lambda k, c: eight(length - 8 - 8 * k, *c, False)[0], carry
    )
    coefs = product * last_follow
    product = product * last_decay
    seg_ref[0] = partial
    seg_ref[1] = product
    seg_ref[2] = coefs
    s = SEG - 1
    own, kept, coef = partial[s:], product[s:], coefs[s:]
    for s in range(SEG - 2, -1, -1):
        factor = product[s : s + 1]
        own = partial[s : s + 1] + factor * own
        kept = factor * kept
        coef = factor * coef
    lines = jnp.concatenate([own, kept, coef, following[0:1]], axis=0)
    all_ref[pl.ds(4 * pl.program_id(0), 4), :] = lines


def columns(*lead):
    return pl.BlockSpec((*lead, LANES), lambda j: (*(0 for _ in lead), j))


def segmented(block):
    steps, envs = block.shape
    return block.reshape(SEG, steps // SEG, envs)


def summary(here, rewards, values, *rest):
    steps, envs = rewards.shape
    groups = envs // LANES
    return pl.pallas_call(
        summary_body,
        grid=(groups,),
        in_specs=[
            SMEM, columns(SEG, steps // SEG), columns(SEG, steps // SEG),
            *(columns(len(part)) for part in rest),
        ],
        out_specs=[columns(3, SEG), pl.BlockSpec((4 * groups, LANES), lambda j: (0, 0))],
        out_shape=[
            jax.ShapeDtypeStruct((3, SEG, envs), F32),
            jax.ShapeDtypeStruct((4 * groups, LANES), F32),
        ],
        compiler_params=params(),
        cost_estimate=cost(16 * steps * envs, 8 * steps * envs),
        name="summary",
    )(here, segmented(rewards), segmented(values), *rest)


def advantage_body(
    here_ref, rew_ref, val_ref, done_ref, taken_ref, discount_ref, retention_ref,
    last_ref, seg_ref, every_ref, adv_ref, stat_ref,
):
    length = rew_ref.shape[1]
    group = pl.program_id(0)
    here = here_ref[2]
    step = stepper(here_ref, done_ref, taken_ref, discount_ref, retention_ref, length)

    boundary = last_ref[...]
    incoming = jnp.zeros((1, LANES), F32)
    for s in range(every_ref.shape[0] - 1, 0, -1):
        lines = every_ref[s, pl.ds(4 * group, 4), :]
        later = here < s
        start = (lines[0:1] + lines[2:3] * boundary) + lines[1:2] * incoming
        incoming = jnp.where(later, start, incoming)
        boundary = jnp.where(later, lines[3:4], boundary)

    partial, product = seg_ref[0], seg_ref[1]
    after = [incoming]
    for s in range(SEG - 1, 0, -1):
        own = partial[s : s + 1]
        if s == SEG - 1:
            own = own + seg_ref[2, s : s + 1, :] * boundary
        after.append(own + product[s : s + 1] * after[-1])
    after = jnp.concatenate(after[::-1], axis=0)

    def body(k, carry):
        later, following, sum_adv, sum_val = carry
        at = length - 8 - 8 * k
        rewards, values = by_step(rew_ref, at), by_step(val_ref, at)
        found = []
        for k in range(7, -1, -1):
            td_error, decay, _ = step(at + k, rewards[k], values[k], following)
            later = td_error + decay * later
            following = values[k]
            found.append(later)
            sum_adv, sum_val = sum_adv + later, sum_val + following
        found = jnp.stack(found[::-1], axis=0)
        adv_ref[:, pl.ds(pl.multiple_of(at, 8), 8), :] = jnp.swapaxes(found, 0, 1)
        return later, following, sum_adv, sum_val

    zero = jnp.zeros((SEG, LANES), F32)
    start = (after, value_after(val_ref, boundary), zero, zero)
    _, _, sum_adv, sum_val = lax.fori_loop(0, length // 8, body, start)
    sums = [jnp.sum(sum_adv), jnp.sum(sum_adv + sum_val)]
    mean_adv, mean_ret = [total / (SEG * length * LANES) for total in sums]

    zero = jnp.zeros((length, LANES), F32)

    def spread(k, carry):
        sq_adv, sq_ret = carry
        own = adv_ref[k]
        off_adv = own - mean_adv
        off_ret = (own + val_ref[k]) - mean_ret
        return sq_adv + off_adv * off_adv, sq_ret + off_ret * off_ret

    sq_adv, sq_ret = lax.fori_loop(0, SEG, spread, (zero, zero), unroll=2)
    sums += [jnp.sum(sq_adv), jnp.sum(sq_ret)]
    lane = lax.broadcasted_iota(jnp.int32, stat_ref.shape, 1)

    @pl.when(group == 0)
    def _():
        stat_ref[...] = jnp.zeros(stat_ref.shape, F32)

    line = stat_ref[...]
    for k, total in enumerate(sums):
        line = jnp.where(lane == 4 * group + k, total, line)
    stat_ref[...] = line


def advantage(here, rewards, values, rest, last_value, segments, every):
    steps, envs = rewards.shape
    adv, stats = pl.pallas_call(
        advantage_body,
        grid=(envs // LANES,),
        in_specs=[
            SMEM, columns(SEG, steps // SEG), columns(SEG, steps // SEG),
            *(columns(len(part)) for part in rest), columns(1), columns(3, SEG), pl.BlockSpec(every.shape, lambda j: (0, 0, 0)),
        ],
        out_specs=[columns(SEG, steps // SEG), pl.BlockSpec((8, LANES), lambda j: (0, 0))],
        out_shape=[
            jax.ShapeDtypeStruct((SEG, steps // SEG, envs), F32),
            jax.ShapeDtypeStruct((8, LANES), F32),
        ],
        compiler_params=params(),
        cost_estimate=cost(24 * steps * envs, 12 * steps * envs),
        name="advantage",
    )(here, segmented(rewards), segmented(values), *rest, last_value, segments, every)
    return adv.reshape(steps, envs), stats


def merged(states, count):
    lane = lax.broadcasted_iota(jnp.int32, states[0].shape, 1)
    mean = sum(states[1:], states[0]) / len(states)
    gaps = [(state - mean) * (state - mean) for state in states]
    gaps = pltpu.roll(sum(gaps[1:], gaps[0]), 2, 1)
    square = sum(states[1:], states[0]) + count * gaps
    return jnp.where(lane < 2, mean, jnp.where(lane < 4, square, 0.0))


def gather_body(groups, count, part_ref, o_ref):
    sums = part_ref[:, 0, :]
    lane = lax.broadcasted_iota(jnp.int32, sums.shape, 1)
    kind = lane % 4

    def total(k, values):
        return jnp.sum(jnp.where((kind == k) & (lane < 4 * groups), values, 0.0))

    whole = count * groups * sums.shape[0]
    means = [total(k, sums) / whole for k in range(2)]
    off = sums / count - jnp.where(kind == 0, means[0], means[1])
    off = count * off * off
    squares = [total(k + 2, sums) + total(k, off) for k in range(2)]
    lane = lax.broadcasted_iota(jnp.int32, o_ref.shape, 1)
    line = jnp.zeros(o_ref.shape, F32)
    for k, value in enumerate(means + squares):
        line = jnp.where(lane == k, value, line)
    o_ref[...] = line


def gathered(adv, rows, groups, count):
    blocks = adv.shape[0]
    return pl.pallas_call(
        functools.partial(gather_body, groups, float(count)),
        grid=(1,),
        in_specs=[pl.BlockSpec((blocks, 8, LANES), lambda i: (0, rows // 8, 0))],
        out_specs=pl.BlockSpec((8, LANES), lambda i: (0, 0)),
        out_shape=jax.ShapeDtypeStruct((8, LANES), F32),
        compiler_params=params(16),
        cost_estimate=cost(1000, 4096 * blocks),
        name="gathered",
    )(adv)


def merge_body(count, *refs):
    refs[-1][...] = merged([ref[...] for ref in refs[:-1]], count)


def merge(states, count):
    return pl.pallas_call(
        functools.partial(merge_body, float(count)),
        in_specs=[VMEM] * len(states),
        out_specs=VMEM,
        out_shape=jax.ShapeDtypeStruct(states[0].shape, F32),
        compiler_params=params(16),
        cost_estimate=cost(1000, 4096 * len(states)),
        name="merge",
    )(*states)


def around(state, axis):
    size = lax.axis_size(axis)
    return [state] + [
        lax.ppermute(state, axis, [(i, (i + far) % size) for i in range(size)])
        for far in range(1, size)
    ]


def normal_body(parts, n_states, count, steps, offset, *refs):
    states, adv = refs[:n_states], refs[n_states]
    vals = refs[n_states + 1 : n_states + 1 + len(parts)]
    out_adv, out_ret, oabuf, orbuf, out_sem = refs[-5:]
    blocks, own, width = oabuf.shape

    state = merged([ref[...] for ref in states], count)
    scale = 1.0 / jnp.sqrt(state / (count * n_states) + 1e-05)
    first = lax.broadcasted_iota(jnp.int32, state.shape, 0) == 0
    lane = lax.broadcasted_iota(jnp.int32, state.shape, 1)
    pick = lambda values, k: jnp.sum(jnp.where(first & (lane == k), values, 0.0))
    mean_adv, mean_ret = pick(state, 0), pick(state, 1)
    scale_adv, scale_ret = pick(scale, 2), pick(scale, 3)

    def stores(s):
        place = pl.ds(pl.multiple_of(s * steps + offset, LANES), width)
        return [
            pltpu.make_async_copy(buf.at[s], out.at[:, place], out_sem.at[k, s])
            for k, (buf, out) in enumerate(((oabuf, out_adv), (orbuf, out_ret)))
        ]

    def work(s, carry):
        h = 0
        for val, (begin, end) in zip(vals, parts):
            for at in range(begin, end, own):
                part = adv[s, h * own : (h + 1) * own, :]
                ret = part + val[s, at : at + own, :]
                lanes = slice(h * LANES, (h + 1) * LANES)
                oabuf[s, :, lanes] = (part - mean_adv) * scale_adv
                orbuf[s, :, lanes] = (ret - mean_ret) * scale_ret
                h += 1
        for copy in stores(s):
            copy.start()
        return carry

    def finish(s, carry):
        for copy in stores(s):
            copy.wait()
        return carry

    lax.fori_loop(0, blocks, work, 0)
    lax.fori_loop(0, blocks, finish, 0)


def normalized(states, count, adv, vals, parts, own, steps, offset, into=()):
    blocks, rows = adv.shape[0], sum(end - begin for begin, end in parts)
    shape = jax.ShapeDtypeStruct((own, blocks * steps), F32)
    at = len(states) + 1 + len(vals)
    width = rows // own * LANES
    return pl.pallas_call(
        functools.partial(normal_body, parts, len(states), float(count), steps, offset),
        in_specs=[VMEM] * at + [ANY] * len(into),
        out_specs=[ANY, ANY],
        out_shape=[shape, shape],
        input_output_aliases={at + k: k for k in range(len(into))},
        scratch_shapes=[
            pltpu.VMEM((blocks, own, width), F32),
            pltpu.VMEM((blocks, own, width), F32),
            pltpu.SemaphoreType.DMA((2, blocks)),
        ],
        compiler_params=params(20),
        cost_estimate=cost(4 * blocks * rows * LANES, 16 * blocks * rows * LANES),
        name="normalized",
    )(*states, adv, *vals, *into)


def exchange(packed, behind=None):
    if behind is not None:
        packed, behind = lax.optimization_barrier((packed, behind))
    return lax.all_to_all(packed, TM, 0, 0, tiled=True), behind


def shards(rewards, values, last_value, done_steps, horizon_offset, discount_rate, trace_rate):
    steps, envs = rewards.shape
    blocks = lax.axis_size(TM)
    here = lax.axis_index(TM)
    horizon = steps * blocks // 2
    groups = envs // LANES
    own = envs // blocks
    one, two, cut = 512, 512, 1024
    rows = lambda count: count // LANES * own

    discount = jnp.exp(-discount_rate)
    retention = discount * jnp.exp(-trace_rate)
    rest = (done_steps.T, horizon_offset[None], discount[None], retention[None])
    where = jnp.stack([here * steps, jnp.int32(horizon), here])

    core = lax.axis_index(ENV[1])
    given = (where, rewards, values, *rest)
    blank = lambda *_: (
        jnp.zeros((3, SEG, envs), F32),
        jnp.zeros((4 * groups, LANES), F32),
    )
    ahead = lax.cond(core == 0, lambda *x: tuple(summary(*x)), blank, *given)
    values_1, ahead = lax.optimization_barrier((values, ahead))
    packed, ahead = lax.optimization_barrier((pack(values_1, blocks, 0, one), ahead))
    val_1, _ = exchange(packed)
    segments, whole = lax.cond(
        core == 0, lambda done, *_: done, lambda _, *x: tuple(summary(*x)), ahead, *given
    )

    val_2, val_1 = exchange(pack(values, blocks, one, two, whole), val_1)
    val_3, val_2 = exchange(pack(values, blocks, one + two, steps - one - two), val_2)
    every = val_2[:, rows(two) :, :]
    adv, local = advantage(
        where, rewards, values, rest, last_value[None], segments, every
    )
    adv_1, val_3 = exchange(pack(adv, blocks, 0, cut, local), val_3)
    adv_2, adv_1 = exchange(pack(adv, blocks, cut, steps - cut), adv_1)

    count = steps * LANES
    state = gathered(adv_1, rows(cut), groups, count)
    count = count * groups * blocks
    state = merge(around(state, ENV[0]), count)
    count = count * lax.axis_size(ENV[0])
    states = around(state, ENV[1])

    held = ((val_1, 0, one), (val_2, one, one + two), (val_3, one + two, steps))

    def write(adv, begin, end, into=()):
        taken = [(val, max(lo, begin) - lo, min(hi, end) - lo) for val, lo, hi in held]
        taken = [part for part in taken if part[1] < part[2]]
        vals = tuple(val for val, _, _ in taken)
        parts = tuple((rows(lo), rows(hi)) for _, lo, hi in taken)
        return normalized(states, count, adv, vals, parts, own, steps, begin, into)

    return tuple(write(adv_2, cut, steps, write(adv_1, 0, cut)))


def solution(mesh):
    split = Mesh(mesh.devices.reshape(4, 4, 4, 2), ALL)
    placed = (P(TM, ENV), P(TM, ENV), P(ENV), P(ENV, None), P(ENV), P(ENV), P(ENV))
    return jax.shard_map(
        shards,
        mesh=split,
        in_specs=placed,
        out_specs=(P(ENV_TM, None), P(ENV_TM, None)),
        check_vma=False,
    )
```

```python
import functools

import jax
import jax.numpy as jnp
from jax import lax
from jax.experimental import pallas as pl
from jax.experimental.pallas import tpu as pltpu
from jax.sharding import Mesh
from jax.sharding import PartitionSpec as P

TM = ("tm_0", "tm_1")
ENV = ("env_0", "env_1")
ALL = ("tm_0", "tm_1", "env_0", "env_1")
ENV_TM = ("env_0", "env_1", "tm_0", "tm_1")
F32 = jnp.float32
LANES = 128
SEG = 32
ROWS = 128
SMEM = pl.BlockSpec(memory_space=pltpu.SMEM)
ANY = pl.BlockSpec(memory_space=pl.ANY)
VMEM = pl.BlockSpec(memory_space=pltpu.VMEM)


def params(mib=56):
    return pltpu.CompilerParams(vmem_limit_bytes=mib << 20)


def cost(flops, moved):
    return pl.CostEstimate(flops=flops, transcendentals=0, bytes_accessed=moved)


def pack_body(dests, riders, *refs):
    x_ref, o_ref = refs[0], refs[-1]
    own = x_ref.shape[1] // dests
    base = pl.program_id(0) * (ROWS // LANES) * own if riders else 0
    for h in range(ROWS // LANES):
        tile = x_ref[h * LANES : (h + 1) * LANES, :].T.reshape(dests, own, LANES)
        if riders:
            o_ref[:, pl.ds(pl.multiple_of(base + h * own, own), own), :] = tile
        else:
            o_ref[:, h * own : (h + 1) * own, :] = tile
    if riders:

        @pl.when(pl.program_id(0) == 0)
        def _():
            lines = refs[1][...]
            o_ref[:, o_ref.shape[1] - riders :, :] = jnp.broadcast_to(
                lines[None], (dests, *lines.shape)
            )


def pack(block, dests, start, count, rider=None):
    envs = block.shape[1]
    own = envs // dests
    riders = 0 if rider is None else rider.shape[0]
    rows = count // LANES * own
    per = ROWS // LANES * own
    in_specs = [pl.BlockSpec((ROWS, envs), lambda i: (start // ROWS + i, 0))]
    if riders:
        in_specs.append(pl.BlockSpec(rider.shape, lambda i: (0, 0)))
        out_spec = pl.BlockSpec((dests, rows + riders, LANES), lambda i: (0, 0, 0))
    else:
        out_spec = pl.BlockSpec((dests, per, LANES), lambda i: (0, i, 0))
    return pl.pallas_call(
        functools.partial(pack_body, dests, riders),
        grid=(count // ROWS,),
        in_specs=in_specs,
        out_specs=out_spec,
        out_shape=jax.ShapeDtypeStruct((dests, rows + riders, LANES), F32),
        compiler_params=params(),
        cost_estimate=cost(0, 8 * count * envs),
        name="pack",
    )(block, *(() if rider is None else (rider,)))


def stepper(here_ref, done_ref, taken_ref, discount_ref, retention_ref, length):
    first = lax.broadcasted_iota(jnp.int32, (SEG, LANES), 0) * length
    start, horizon = here_ref[0], here_ref[1]
    marks = [done_ref[k : k + 1, :] - start for k in range(done_ref.shape[0])]
    full = horizon - 1 - taken_ref[...] - start
    for _ in range(2):
        full = jnp.where(full < 0, full + horizon, full)
    marks.append(full)
    discount, retention = discount_ref[...], retention_ref[...]

    def step(i, reward, value, next_value):
        time = first + i
        ended = marks[0] == time
        for mark in marks[1:-1]:
            ended = ended | (mark == time)
        follow = jnp.where(ended, 0.0, discount)
        decay = jnp.where(ended | (marks[-1] == time), 0.0, retention)
        return reward + follow * next_value - value, decay, follow

    return step


def by_step(ref, at):
    return jnp.swapaxes(ref[:, pl.ds(pl.multiple_of(at, 8), 8), :], 0, 1)


def value_after(val_ref, boundary):
    firsts = jnp.swapaxes(val_ref[:, 0:8, :], 0, 1)[0]
    return jnp.concatenate([firsts[1:], boundary], axis=0)


def summary_body(here_ref, rew_ref, val_ref, *refs):
    seg_ref, all_ref = refs[-2:]
    length = rew_ref.shape[1]
    step = stepper(here_ref, *refs[:4], length)
    zero = jnp.zeros((SEG, LANES), F32)

    def eight(at, partial, product, following, last):
        rewards, values = by_step(rew_ref, at), by_step(val_ref, at)
        for k in range(7, -1, -1):
            td_error, decay, follow = step(at + k, rewards[k], values[k], following)
            if last and k == 7:
                partial, kept = td_error, (decay, follow)
            else:
                partial, product = td_error + decay * partial, decay * product
            following = values[k]
        return (partial, product, following), (kept if last else None)

    carry, (last_decay, last_follow) = eight(
        length - 8, zero, zero + 1.0, value_after(val_ref, zero[:1]), True
    )
    partial, product, following = lax.fori_loop(
        1, length // 8, lambda k, c: eight(length - 8 - 8 * k, *c, False)[0], carry
    )
    coefs = product * last_follow
    product = product * last_decay
    seg_ref[0] = partial
    seg_ref[1] = product
    seg_ref[2] = coefs
    s = SEG - 1
    own, kept, coef = partial[s:], product[s:], coefs[s:]
    for s in range(SEG - 2, -1, -1):
        factor = product[s : s + 1]
        own = partial[s : s + 1] + factor * own
        kept = factor * kept
        coef = factor * coef
    lines = jnp.concatenate([own, kept, coef, following[0:1]], axis=0)
    all_ref[pl.ds(4 * pl.program_id(0), 4), :] = lines


def columns(*lead):
    return pl.BlockSpec((*lead, LANES), lambda j: (*(0 for _ in lead), j))


def segmented(block):
    steps, envs = block.shape
    return block.reshape(SEG, steps // SEG, envs)


def summary(here, rewards, values, *rest):
    steps, envs = rewards.shape
    groups = envs // LANES
    return pl.pallas_call(
        summary_body,
        grid=(groups,),
        in_specs=[
            SMEM, columns(SEG, steps // SEG), columns(SEG, steps // SEG),
            *(columns(len(part)) for part in rest),
        ],
        out_specs=[columns(3, SEG), pl.BlockSpec((4 * groups, LANES), lambda j: (0, 0))],
        out_shape=[
            jax.ShapeDtypeStruct((3, SEG, envs), F32),
            jax.ShapeDtypeStruct((4 * groups, LANES), F32),
        ],
        compiler_params=params(),
        cost_estimate=cost(16 * steps * envs, 8 * steps * envs),
        name="summary",
    )(here, segmented(rewards), segmented(values), *rest)


def advantage_body(
    here_ref, rew_ref, val_ref, done_ref, taken_ref, discount_ref, retention_ref,
    last_ref, seg_ref, every_ref, adv_ref, stat_ref,
):
    length = rew_ref.shape[1]
    group = pl.program_id(0)
    here = here_ref[2]
    step = stepper(here_ref, done_ref, taken_ref, discount_ref, retention_ref, length)

    boundary = last_ref[...]
    incoming = jnp.zeros((1, LANES), F32)
    for s in range(every_ref.shape[0] - 1, 0, -1):
        lines = every_ref[s, pl.ds(4 * group, 4), :]
        later = here < s
        start = (lines[0:1] + lines[2:3] * boundary) + lines[1:2] * incoming
        incoming = jnp.where(later, start, incoming)
        boundary = jnp.where(later, lines[3:4], boundary)

    partial, product = seg_ref[0], seg_ref[1]
    after = [incoming]
    for s in range(SEG - 1, 0, -1):
        own = partial[s : s + 1]
        if s == SEG - 1:
            own = own + seg_ref[2, s : s + 1, :] * boundary
        after.append(own + product[s : s + 1] * after[-1])
    after = jnp.concatenate(after[::-1], axis=0)

    def body(k, carry):
        later, following, sum_adv, sum_val = carry
        at = length - 8 - 8 * k
        rewards, values = by_step(rew_ref, at), by_step(val_ref, at)
        found = []
        for k in range(7, -1, -1):
            td_error, decay, _ = step(at + k, rewards[k], values[k], following)
            later = td_error + decay * later
            following = values[k]
            found.append(later)
            sum_adv, sum_val = sum_adv + later, sum_val + following
        found = jnp.stack(found[::-1], axis=0)
        adv_ref[:, pl.ds(pl.multiple_of(at, 8), 8), :] = jnp.swapaxes(found, 0, 1)
        return later, following, sum_adv, sum_val

    zero = jnp.zeros((SEG, LANES), F32)
    start = (after, value_after(val_ref, boundary), zero, zero)
    _, _, sum_adv, sum_val = lax.fori_loop(0, length // 8, body, start)
    sums = [jnp.sum(sum_adv), jnp.sum(sum_adv + sum_val)]
    mean_adv, mean_ret = [total / (SEG * length * LANES) for total in sums]

    zero = jnp.zeros((length, LANES), F32)

    def spread(k, carry):
        sq_adv, sq_ret = carry
        own = adv_ref[k]
        off_adv = own - mean_adv
        off_ret = (own + val_ref[k]) - mean_ret
        return sq_adv + off_adv * off_adv, sq_ret + off_ret * off_ret

    sq_adv, sq_ret = lax.fori_loop(0, SEG, spread, (zero, zero), unroll=2)
    sums += [jnp.sum(sq_adv), jnp.sum(sq_ret)]
    lane = lax.broadcasted_iota(jnp.int32, stat_ref.shape, 1)

    @pl.when(group == 0)
    def _():
        stat_ref[...] = jnp.zeros(stat_ref.shape, F32)

    line = stat_ref[...]
    for k, total in enumerate(sums):
        line = jnp.where(lane == 4 * group + k, total, line)
    stat_ref[...] = line


def advantage(here, rewards, values, rest, last_value, segments, every):
    steps, envs = rewards.shape
    adv, stats = pl.pallas_call(
        advantage_body,
        grid=(envs // LANES,),
        in_specs=[
            SMEM, columns(SEG, steps // SEG), columns(SEG, steps // SEG),
            *(columns(len(part)) for part in rest), columns(1), columns(3, SEG), pl.BlockSpec(every.shape, lambda j: (0, 0, 0)),
        ],
        out_specs=[columns(SEG, steps // SEG), pl.BlockSpec((8, LANES), lambda j: (0, 0))],
        out_shape=[
            jax.ShapeDtypeStruct((SEG, steps // SEG, envs), F32),
            jax.ShapeDtypeStruct((8, LANES), F32),
        ],
        compiler_params=params(),
        cost_estimate=cost(24 * steps * envs, 12 * steps * envs),
        name="advantage",
    )(here, segmented(rewards), segmented(values), *rest, last_value, segments, every)
    return adv.reshape(steps, envs), stats


def merged(states, count):
    lane = lax.broadcasted_iota(jnp.int32, states[0].shape, 1)
    mean = sum(states[1:], states[0]) / len(states)
    gaps = [(state - mean) * (state - mean) for state in states]
    gaps = pltpu.roll(sum(gaps[1:], gaps[0]), 2, 1)
    square = sum(states[1:], states[0]) + count * gaps
    return jnp.where(lane < 2, mean, jnp.where(lane < 4, square, 0.0))


def gather_body(groups, count, part_ref, o_ref):
    sums = part_ref[:, 0, :]
    lane = lax.broadcasted_iota(jnp.int32, sums.shape, 1)
    kind = lane % 4

    def total(k, values):
        return jnp.sum(jnp.where((kind == k) & (lane < 4 * groups), values, 0.0))

    whole = count * groups * sums.shape[0]
    means = [total(k, sums) / whole for k in range(2)]
    off = sums / count - jnp.where(kind == 0, means[0], means[1])
    off = count * off * off
    squares = [total(k + 2, sums) + total(k, off) for k in range(2)]
    lane = lax.broadcasted_iota(jnp.int32, o_ref.shape, 1)
    line = jnp.zeros(o_ref.shape, F32)
    for k, value in enumerate(means + squares):
        line = jnp.where(lane == k, value, line)
    o_ref[...] = line


def gathered(adv, rows, groups, count):
    blocks = adv.shape[0]
    return pl.pallas_call(
        functools.partial(gather_body, groups, float(count)),
        grid=(1,),
        in_specs=[pl.BlockSpec((blocks, 8, LANES), lambda i: (0, rows // 8, 0))],
        out_specs=pl.BlockSpec((8, LANES), lambda i: (0, 0)),
        out_shape=jax.ShapeDtypeStruct((8, LANES), F32),
        compiler_params=params(16),
        cost_estimate=cost(1000, 4096 * blocks),
        name="gathered",
    )(adv)


def merge_body(count, *refs):
    refs[-1][...] = merged([ref[...] for ref in refs[:-1]], count)


def merge(states, count):
    return pl.pallas_call(
        functools.partial(merge_body, float(count)),
        in_specs=[VMEM] * len(states),
        out_specs=VMEM,
        out_shape=jax.ShapeDtypeStruct(states[0].shape, F32),
        compiler_params=params(16),
        cost_estimate=cost(1000, 4096 * len(states)),
        name="merge",
    )(*states)


def around(state, axis):
    size = lax.axis_size(axis)
    return [state] + [
        lax.ppermute(state, axis, [(i, (i + far) % size) for i in range(size)])
        for far in range(1, size)
    ]


def normal_body(parts, n_states, count, steps, offset, *refs):
    states, adv = refs[:n_states], refs[n_states]
    vals = refs[n_states + 1 : n_states + 1 + len(parts)]
    out_adv, out_ret, oabuf, orbuf, out_sem = refs[-5:]
    blocks, own, width = oabuf.shape

    state = merged([ref[...] for ref in states], count)
    scale = 1.0 / jnp.sqrt(state / (count * n_states) + 1e-05)
    first = lax.broadcasted_iota(jnp.int32, state.shape, 0) == 0
    lane = lax.broadcasted_iota(jnp.int32, state.shape, 1)
    pick = lambda values, k: jnp.sum(jnp.where(first & (lane == k), values, 0.0))
    mean_adv, mean_ret = pick(state, 0), pick(state, 1)
    scale_adv, scale_ret = pick(scale, 2), pick(scale, 3)

    def stores(s):
        place = pl.ds(pl.multiple_of(s * steps + offset, LANES), width)
        return [
            pltpu.make_async_copy(buf.at[s], out.at[:, place], out_sem.at[k, s])
            for k, (buf, out) in enumerate(((oabuf, out_adv), (orbuf, out_ret)))
        ]

    def work(s, carry):
        h = 0
        for val, (begin, end) in zip(vals, parts):
            for at in range(begin, end, own):
                part = adv[s, h * own : (h + 1) * own, :]
                ret = part + val[s, at : at + own, :]
                lanes = slice(h * LANES, (h + 1) * LANES)
                oabuf[s, :, lanes] = (part - mean_adv) * scale_adv
                orbuf[s, :, lanes] = (ret - mean_ret) * scale_ret
                h += 1
        for copy in stores(s):
            copy.start()
        return carry

    def finish(s, carry):
        for copy in stores(s):
            copy.wait()
        return carry

    lax.fori_loop(0, blocks, work, 0)
    lax.fori_loop(0, blocks, finish, 0)


def normalized(states, count, adv, vals, parts, own, steps, offset, into=()):
    blocks, rows = adv.shape[0], sum(end - begin for begin, end in parts)
    shape = jax.ShapeDtypeStruct((own, blocks * steps), F32)
    at = len(states) + 1 + len(vals)
    width = rows // own * LANES
    return pl.pallas_call(
        functools.partial(normal_body, parts, len(states), float(count), steps, offset),
        in_specs=[VMEM] * at + [ANY] * len(into),
        out_specs=[ANY, ANY],
        out_shape=[shape, shape],
        input_output_aliases={at + k: k for k in range(len(into))},
        scratch_shapes=[
            pltpu.VMEM((blocks, own, width), F32),
            pltpu.VMEM((blocks, own, width), F32),
            pltpu.SemaphoreType.DMA((2, blocks)),
        ],
        compiler_params=params(20),
        cost_estimate=cost(4 * blocks * rows * LANES, 16 * blocks * rows * LANES),
        name="normalized",
    )(*states, adv, *vals, *into)


def exchange(packed, behind=None):
    if behind is not None:
        packed, behind = lax.optimization_barrier((packed, behind))
    return lax.all_to_all(packed, TM, 0, 0, tiled=True), behind


def shards(rewards, values, last_value, done_steps, horizon_offset, discount_rate, trace_rate):
    steps, envs = rewards.shape
    blocks = lax.axis_size(TM)
    here = lax.axis_index(TM)
    horizon = steps * blocks // 2
    groups = envs // LANES
    own = envs // blocks
    one, two, cut = 512, 512, 1024
    rows = lambda count: count // LANES * own

    discount = jnp.exp(-discount_rate)
    retention = discount * jnp.exp(-trace_rate)
    rest = (done_steps.T, horizon_offset[None], discount[None], retention[None])
    where = jnp.stack([here * steps, jnp.int32(horizon), here])

    core = lax.axis_index(ENV[1])
    given = (where, rewards, values, *rest)
    blank = lambda *_: (
        jnp.zeros((3, SEG, envs), F32),
        jnp.zeros((4 * groups, LANES), F32),
    )
    ahead = lax.cond(core == 0, lambda *x: tuple(summary(*x)), blank, *given)
    values_1, ahead = lax.optimization_barrier((values, ahead))
    packed, ahead = lax.optimization_barrier((pack(values_1, blocks, 0, one), ahead))
    val_1, _ = exchange(packed)
    segments, whole = lax.cond(
        core == 0, lambda done, *_: done, lambda _, *x: tuple(summary(*x)), ahead, *given
    )

    val_2, val_1 = exchange(pack(values, blocks, one, two, whole), val_1)
    val_3, val_2 = exchange(pack(values, blocks, one + two, steps - one - two), val_2)
    every = val_2[:, rows(two) :, :]
    adv, local = advantage(
        where, rewards, values, rest, last_value[None], segments, every
    )
    adv_1, val_3 = exchange(pack(adv, blocks, 0, cut, local), val_3)
    adv_2, adv_1 = exchange(pack(adv, blocks, cut, steps - cut), adv_1)

    count = steps * LANES
    state = gathered(adv_1, rows(cut), groups, count)
    count = count * groups * blocks
    state = merge(around(state, ENV[0]), count)
    count = count * lax.axis_size(ENV[0])
    states = around(state, ENV[1])

    held = ((val_1, 0, one), (val_2, one, one + two), (val_3, one + two, steps))

    def write(adv, begin, end, into=()):
        taken = [(val, max(lo, begin) - lo, min(hi, end) - lo) for val, lo, hi in held]
        taken = [part for part in taken if part[1] < part[2]]
        vals = tuple(val for val, _, _ in taken)
        parts = tuple((rows(lo), rows(hi)) for _, lo, hi in taken)
        return normalized(states, count, adv, vals, parts, own, steps, begin, into)

    return tuple(write(adv_2, cut, steps, write(adv_1, 0, cut)))


def solution(mesh):
    split = Mesh(mesh.devices.reshape(4, 4, 4, 2), ALL)
    placed = (P(TM, ENV), P(TM, ENV), P(ENV), P(ENV, None), P(ENV), P(ENV), P(ENV))
    return jax.shard_map(
        shards,
        mesh=split,
        in_specs=placed,
        out_specs=(P(ENV_TM, None), P(ENV_TM, None)),
        check_vma=False,
    )
```

```python
import functools

import jax
import jax.numpy as jnp
from jax import lax
from jax.experimental import pallas as pl
from jax.experimental.pallas import tpu as pltpu
from jax.sharding import Mesh
from jax.sharding import PartitionSpec as P

TM = ("tm_0", "tm_1")
ENV = ("env_0", "env_1")
ALL = ("tm_0", "tm_1", "env_0", "env_1")
ENV_TM = ("env_0", "env_1", "tm_0", "tm_1")
F32 = jnp.float32
LANES = 128
SEG = 32
ROWS = 512
SMEM = pl.BlockSpec(memory_space=pltpu.SMEM)
ANY = pl.BlockSpec(memory_space=pl.ANY)
VMEM = pl.BlockSpec(memory_space=pltpu.VMEM)


def params(mib=56):
    return pltpu.CompilerParams(vmem_limit_bytes=mib << 20)


def cost(flops, moved):
    return pl.CostEstimate(flops=flops, transcendentals=0, bytes_accessed=moved)


def pack_body(dests, riders, *refs):
    x_ref, o_ref = refs[0], refs[-1]
    own = x_ref.shape[1] // dests
    base = pl.program_id(0) * (ROWS // LANES) * own if riders else 0
    for h in range(ROWS // LANES):
        tile = x_ref[h * LANES : (h + 1) * LANES, :].T.reshape(dests, own, LANES)
        if riders:
            o_ref[:, pl.ds(pl.multiple_of(base + h * own, own), own), :] = tile
        else:
            o_ref[:, h * own : (h + 1) * own, :] = tile
    if riders:

        @pl.when(pl.program_id(0) == 0)
        def _():
            lines = refs[1][...]
            o_ref[:, o_ref.shape[1] - riders :, :] = jnp.broadcast_to(
                lines[None], (dests, *lines.shape)
            )


def pack(block, dests, start, count, rider=None):
    envs = block.shape[1]
    own = envs // dests
    riders = 0 if rider is None else rider.shape[0]
    rows = count // LANES * own
    per = ROWS // LANES * own
    in_specs = [pl.BlockSpec((ROWS, envs), lambda i: (start // ROWS + i, 0))]
    if riders:
        in_specs.append(pl.BlockSpec(rider.shape, lambda i: (0, 0)))
        out_spec = pl.BlockSpec((dests, rows + riders, LANES), lambda i: (0, 0, 0))
    else:
        out_spec = pl.BlockSpec((dests, per, LANES), lambda i: (0, i, 0))
    return pl.pallas_call(
        functools.partial(pack_body, dests, riders),
        grid=(count // ROWS,),
        in_specs=in_specs,
        out_specs=out_spec,
        out_shape=jax.ShapeDtypeStruct((dests, rows + riders, LANES), F32),
        compiler_params=params(),
        cost_estimate=cost(0, 8 * count * envs),
        name="pack",
    )(block, *(() if rider is None else (rider,)))


def stepper(here_ref, done_ref, taken_ref, discount_ref, retention_ref, length):
    first = lax.broadcasted_iota(jnp.int32, (SEG, LANES), 0) * length
    start, horizon = here_ref[0], here_ref[1]
    marks = [done_ref[k : k + 1, :] - start for k in range(done_ref.shape[0])]
    full = horizon - 1 - taken_ref[...] - start
    for _ in range(2):
        full = jnp.where(full < 0, full + horizon, full)
    marks.append(full)
    discount, retention = discount_ref[...], retention_ref[...]

    def step(i, reward, value, next_value):
        time = first + i
        ended = marks[0] == time
        for mark in marks[1:-1]:
            ended = ended | (mark == time)
        follow = jnp.where(ended, 0.0, discount)
        decay = jnp.where(ended | (marks[-1] == time), 0.0, retention)
        return reward + follow * next_value - value, decay, follow

    return step


def by_step(ref, at):
    return jnp.swapaxes(ref[:, pl.ds(pl.multiple_of(at, 8), 8), :], 0, 1)


def value_after(val_ref, boundary):
    firsts = jnp.swapaxes(val_ref[:, 0:8, :], 0, 1)[0]
    return jnp.concatenate([firsts[1:], boundary], axis=0)


def summary_body(here_ref, rew_ref, val_ref, *refs):
    seg_ref, all_ref = refs[-2:]
    length = rew_ref.shape[1]
    step = stepper(here_ref, *refs[:4], length)
    zero = jnp.zeros((SEG, LANES), F32)

    def eight(at, partial, product, following, last):
        rewards, values = by_step(rew_ref, at), by_step(val_ref, at)
        for k in range(7, -1, -1):
            td_error, decay, follow = step(at + k, rewards[k], values[k], following)
            if last and k == 7:
                partial, kept = td_error, (decay, follow)
            else:
                partial, product = td_error + decay * partial, decay * product
            following = values[k]
        return (partial, product, following), (kept if last else None)

    carry, (last_decay, last_follow) = eight(
        length - 8, zero, zero + 1.0, value_after(val_ref, zero[:1]), True
    )
    partial, product, following = lax.fori_loop(
        1, length // 8, lambda k, c: eight(length - 8 - 8 * k, *c, False)[0], carry
    )
    coefs = product * last_follow
    product = product * last_decay
    seg_ref[0] = partial
    seg_ref[1] = product
    seg_ref[2] = coefs
    s = SEG - 1
    own, kept, coef = partial[s:], product[s:], coefs[s:]
    for s in range(SEG - 2, -1, -1):
        factor = product[s : s + 1]
        own = partial[s : s + 1] + factor * own
        kept = factor * kept
        coef = factor * coef
    lines = jnp.concatenate([own, kept, coef, following[0:1]], axis=0)
    all_ref[pl.ds(4 * pl.program_id(0), 4), :] = lines


def columns(*lead):
    return pl.BlockSpec((*lead, LANES), lambda j: (*(0 for _ in lead), j))


def segmented(block):
    steps, envs = block.shape
    return block.reshape(SEG, steps // SEG, envs)


def summary(here, rewards, values, *rest):
    steps, envs = rewards.shape
    groups = envs // LANES
    return pl.pallas_call(
        summary_body,
        grid=(groups,),
        in_specs=[
            SMEM, columns(SEG, steps // SEG), columns(SEG, steps // SEG),
            *(columns(len(part)) for part in rest),
        ],
        out_specs=[columns(3, SEG), pl.BlockSpec((4 * groups, LANES), lambda j: (0, 0))],
        out_shape=[
            jax.ShapeDtypeStruct((3, SEG, envs), F32),
            jax.ShapeDtypeStruct((4 * groups, LANES), F32),
        ],
        compiler_params=params(),
        cost_estimate=cost(16 * steps * envs, 8 * steps * envs),
        name="summary",
    )(here, segmented(rewards), segmented(values), *rest)


def advantage_body(
    here_ref, rew_ref, val_ref, done_ref, taken_ref, discount_ref, retention_ref,
    last_ref, seg_ref, every_ref, adv_ref, stat_ref,
):
    length = rew_ref.shape[1]
    group = pl.program_id(0)
    here = here_ref[2]
    step = stepper(here_ref, done_ref, taken_ref, discount_ref, retention_ref, length)

    boundary = last_ref[...]
    incoming = jnp.zeros((1, LANES), F32)
    for s in range(every_ref.shape[0] - 1, 0, -1):
        lines = every_ref[s, pl.ds(4 * group, 4), :]
        later = here < s
        start = (lines[0:1] + lines[2:3] * boundary) + lines[1:2] * incoming
        incoming = jnp.where(later, start, incoming)
        boundary = jnp.where(later, lines[3:4], boundary)

    partial, product = seg_ref[0], seg_ref[1]
    after = [incoming]
    for s in range(SEG - 1, 0, -1):
        own = partial[s : s + 1]
        if s == SEG - 1:
            own = own + seg_ref[2, s : s + 1, :] * boundary
        after.append(own + product[s : s + 1] * after[-1])
    after = jnp.concatenate(after[::-1], axis=0)

    def body(k, carry):
        later, following, sum_adv, sum_val = carry
        at = length - 8 - 8 * k
        rewards, values = by_step(rew_ref, at), by_step(val_ref, at)
        found = []
        for k in range(7, -1, -1):
            td_error, decay, _ = step(at + k, rewards[k], values[k], following)
            later = td_error + decay * later
            following = values[k]
            found.append(later)
            sum_adv, sum_val = sum_adv + later, sum_val + following
        found = jnp.stack(found[::-1], axis=0)
        adv_ref[:, pl.ds(pl.multiple_of(at, 8), 8), :] = jnp.swapaxes(found, 0, 1)
        return later, following, sum_adv, sum_val

    zero = jnp.zeros((SEG, LANES), F32)
    start = (after, value_after(val_ref, boundary), zero, zero)
    _, _, sum_adv, sum_val = lax.fori_loop(0, length // 8, body, start)
    sums = [jnp.sum(sum_adv), jnp.sum(sum_adv + sum_val)]
    mean_adv, mean_ret = [total / (SEG * length * LANES) for total in sums]

    zero = jnp.zeros((length, LANES), F32)

    def spread(k, carry):
        sq_adv, sq_ret = carry
        own = adv_ref[k]
        off_adv = own - mean_adv
        off_ret = (own + val_ref[k]) - mean_ret
        return sq_adv + off_adv * off_adv, sq_ret + off_ret * off_ret

    sq_adv, sq_ret = lax.fori_loop(0, SEG, spread, (zero, zero), unroll=2)
    sums += [jnp.sum(sq_adv), jnp.sum(sq_ret)]
    lane = lax.broadcasted_iota(jnp.int32, stat_ref.shape, 1)

    @pl.when(group == 0)
    def _():
        stat_ref[...] = jnp.zeros(stat_ref.shape, F32)

    line = stat_ref[...]
    for k, total in enumerate(sums):
        line = jnp.where(lane == 4 * group + k, total, line)
    stat_ref[...] = line


def advantage(here, rewards, values, rest, last_value, segments, every):
    steps, envs = rewards.shape
    adv, stats = pl.pallas_call(
        advantage_body,
        grid=(envs // LANES,),
        in_specs=[
            SMEM, columns(SEG, steps // SEG), columns(SEG, steps // SEG),
            *(columns(len(part)) for part in rest), columns(1), columns(3, SEG), pl.BlockSpec(every.shape, lambda j: (0, 0, 0)),
        ],
        out_specs=[columns(SEG, steps // SEG), pl.BlockSpec((8, LANES), lambda j: (0, 0))],
        out_shape=[
            jax.ShapeDtypeStruct((SEG, steps // SEG, envs), F32),
            jax.ShapeDtypeStruct((8, LANES), F32),
        ],
        compiler_params=params(),
        cost_estimate=cost(24 * steps * envs, 12 * steps * envs),
        name="advantage",
    )(here, segmented(rewards), segmented(values), *rest, last_value, segments, every)
    return adv.reshape(steps, envs), stats


def merged(states, count):
    lane = lax.broadcasted_iota(jnp.int32, states[0].shape, 1)
    mean = sum(states[1:], states[0]) / len(states)
    gaps = [(state - mean) * (state - mean) for state in states]
    gaps = pltpu.roll(sum(gaps[1:], gaps[0]), 2, 1)
    square = sum(states[1:], states[0]) + count * gaps
    return jnp.where(lane < 2, mean, jnp.where(lane < 4, square, 0.0))


def gather_body(groups, count, part_ref, o_ref):
    sums = part_ref[:, 0, :]
    lane = lax.broadcasted_iota(jnp.int32, sums.shape, 1)
    kind = lane % 4

    def total(k, values):
        return jnp.sum(jnp.where((kind == k) & (lane < 4 * groups), values, 0.0))

    whole = count * groups * sums.shape[0]
    means = [total(k, sums) / whole for k in range(2)]
    off = sums / count - jnp.where(kind == 0, means[0], means[1])
    off = count * off * off
    squares = [total(k + 2, sums) + total(k, off) for k in range(2)]
    lane = lax.broadcasted_iota(jnp.int32, o_ref.shape, 1)
    line = jnp.zeros(o_ref.shape, F32)
    for k, value in enumerate(means + squares):
        line = jnp.where(lane == k, value, line)
    o_ref[...] = line


def gathered(adv, rows, groups, count):
    blocks = adv.shape[0]
    return pl.pallas_call(
        functools.partial(gather_body, groups, float(count)),
        grid=(1,),
        in_specs=[pl.BlockSpec((blocks, 8, LANES), lambda i: (0, rows // 8, 0))],
        out_specs=pl.BlockSpec((8, LANES), lambda i: (0, 0)),
        out_shape=jax.ShapeDtypeStruct((8, LANES), F32),
        compiler_params=params(16),
        cost_estimate=cost(1000, 4096 * blocks),
        name="gathered",
    )(adv)


def merge_body(count, *refs):
    refs[-1][...] = merged([ref[...] for ref in refs[:-1]], count)


def merge(states, count):
    return pl.pallas_call(
        functools.partial(merge_body, float(count)),
        in_specs=[VMEM] * len(states),
        out_specs=VMEM,
        out_shape=jax.ShapeDtypeStruct(states[0].shape, F32),
        compiler_params=params(16),
        cost_estimate=cost(1000, 4096 * len(states)),
        name="merge",
    )(*states)


def around(state, axis):
    size = lax.axis_size(axis)
    return [state] + [
        lax.ppermute(state, axis, [(i, (i + far) % size) for i in range(size)])
        for far in range(1, size)
    ]


def normal_body(parts, n_states, count, steps, offset, *refs):
    states, adv = refs[:n_states], refs[n_states]
    vals = refs[n_states + 1 : n_states + 1 + len(parts)]
    out_adv, out_ret, oabuf, orbuf, out_sem = refs[-5:]
    blocks, own, width = oabuf.shape

    state = merged([ref[...] for ref in states], count)
    scale = 1.0 / jnp.sqrt(state / (count * n_states) + 1e-05)
    first = lax.broadcasted_iota(jnp.int32, state.shape, 0) == 0
    lane = lax.broadcasted_iota(jnp.int32, state.shape, 1)
    pick = lambda values, k: jnp.sum(jnp.where(first & (lane == k), values, 0.0))
    mean_adv, mean_ret = pick(state, 0), pick(state, 1)
    scale_adv, scale_ret = pick(scale, 2), pick(scale, 3)

    def stores(s):
        place = pl.ds(pl.multiple_of(s * steps + offset, LANES), width)
        return [
            pltpu.make_async_copy(buf.at[s], out.at[:, place], out_sem.at[k, s])
            for k, (buf, out) in enumerate(((oabuf, out_adv), (orbuf, out_ret)))
        ]

    def work(s, carry):
        h = 0
        for val, (begin, end) in zip(vals, parts):
            for at in range(begin, end, own):
                part = adv[s, h * own : (h + 1) * own, :]
                ret = part + val[s, at : at + own, :]
                lanes = slice(h * LANES, (h + 1) * LANES)
                oabuf[s, :, lanes] = (part - mean_adv) * scale_adv
                orbuf[s, :, lanes] = (ret - mean_ret) * scale_ret
                h += 1
        for copy in stores(s):
            copy.start()
        return carry

    def finish(s, carry):
        for copy in stores(s):
            copy.wait()
        return carry

    lax.fori_loop(0, blocks, work, 0)
    lax.fori_loop(0, blocks, finish, 0)


def normalized(states, count, adv, vals, parts, own, steps, offset, into=()):
    blocks, rows = adv.shape[0], sum(end - begin for begin, end in parts)
    shape = jax.ShapeDtypeStruct((own, blocks * steps), F32)
    at = len(states) + 1 + len(vals)
    width = rows // own * LANES
    return pl.pallas_call(
        functools.partial(normal_body, parts, len(states), float(count), steps, offset),
        in_specs=[VMEM] * at + [ANY] * len(into),
        out_specs=[ANY, ANY],
        out_shape=[shape, shape],
        input_output_aliases={at + k: k for k in range(len(into))},
        scratch_shapes=[
            pltpu.VMEM((blocks, own, width), F32),
            pltpu.VMEM((blocks, own, width), F32),
            pltpu.SemaphoreType.DMA((2, blocks)),
        ],
        compiler_params=params(20),
        cost_estimate=cost(4 * blocks * rows * LANES, 16 * blocks * rows * LANES),
        name="normalized",
    )(*states, adv, *vals, *into)


def exchange(packed, behind=None):
    if behind is not None:
        packed, behind = lax.optimization_barrier((packed, behind))
    return lax.all_to_all(packed, TM, 0, 0, tiled=True), behind


def shards(rewards, values, last_value, done_steps, horizon_offset, discount_rate, trace_rate):
    steps, envs = rewards.shape
    blocks = lax.axis_size(TM)
    here = lax.axis_index(TM)
    horizon = steps * blocks // 2
    groups = envs // LANES
    own = envs // blocks
    one, two, cut = 512, 512, 1024
    rows = lambda count: count // LANES * own

    discount = jnp.exp(-discount_rate)
    retention = discount * jnp.exp(-trace_rate)
    rest = (done_steps.T, horizon_offset[None], discount[None], retention[None])
    where = jnp.stack([here * steps, jnp.int32(horizon), here])

    core = lax.axis_index(ENV[1])
    given = (where, rewards, values, *rest)
    blank = lambda *_: (
        jnp.zeros((3, SEG, envs), F32),
        jnp.zeros((4 * groups, LANES), F32),
    )
    ahead = lax.cond(core == 0, lambda *x: tuple(summary(*x)), blank, *given)
    values_1, ahead = lax.optimization_barrier((values, ahead))
    packed, ahead = lax.optimization_barrier((pack(values_1, blocks, 0, one), ahead))
    val_1, _ = exchange(packed)
    segments, whole = lax.cond(
        core == 0, lambda done, *_: done, lambda _, *x: tuple(summary(*x)), ahead, *given
    )

    val_2, val_1 = exchange(pack(values, blocks, one, two, whole), val_1)
    val_3, val_2 = exchange(pack(values, blocks, one + two, steps - one - two), val_2)
    every = val_2[:, rows(two) :, :]
    adv, local = advantage(
        where, rewards, values, rest, last_value[None], segments, every
    )
    adv_1, val_3 = exchange(pack(adv, blocks, 0, cut, local), val_3)
    adv_2, adv_1 = exchange(pack(adv, blocks, cut, steps - cut), adv_1)

    count = steps * LANES
    state = gathered(adv_1, rows(cut), groups, count)
    count = count * groups * blocks
    state = merge(around(state, ENV[0]), count)
    count = count * lax.axis_size(ENV[0])
    states = around(state, ENV[1])

    held = ((val_1, 0, one), (val_2, one, one + two), (val_3, one + two, steps))

    def write(adv, begin, end, into=()):
        taken = [(val, max(lo, begin) - lo, min(hi, end) - lo) for val, lo, hi in held]
        taken = [part for part in taken if part[1] < part[2]]
        vals = tuple(val for val, _, _ in taken)
        parts = tuple((rows(lo), rows(hi)) for _, lo, hi in taken)
        return normalized(states, count, adv, vals, parts, own, steps, begin, into)

    return tuple(write(adv_2, cut, steps, write(adv_1, 0, cut)))


def solution(mesh):
    split = Mesh(mesh.devices.reshape(4, 4, 4, 2), ALL)
    placed = (P(TM, ENV), P(TM, ENV), P(ENV), P(ENV, None), P(ENV), P(ENV), P(ENV))
    return jax.shard_map(
        shards,
        mesh=split,
        in_specs=placed,
        out_specs=(P(ENV_TM, None), P(ENV_TM, None)),
        check_vma=False,
    )
```
